256 devices in a mesh: area: 32 (over y, x, core), pop: 8 (over z).
Axes of the slice: x: 4, y: 4, z: 8, core: 2. Of those that a mesh axis runs over, the one named last changes fastest.
Arguments:
- history: bfloat16 [4, 32, 64, 32, 128], P(None, 'area', 'pop'), may hold values from -1 to 1
- external: bfloat16 [32, 64, 32, 128], P('area', 'pop'), may hold values from -6 to 6
- leak_rate: float32 [32, 64, 128], P('area', 'pop'), may hold values from 0.05 to 1
- intra_index: int32 [32, 64, 32], P('area', 'pop'), may hold values from 0 to 63
- intra_weight: bfloat16 [32, 64, 32, 128, 128], P('area', 'pop'), may hold values from -0.09375 to 0.09375
- inter_pick: int32 [32, 64, 12], P('area', 'pop'), may hold values from 0 to 1
- inter_weight: bfloat16 [32, 64, 12, 128, 128], P('area', 'pop'), may hold values from -0.15625 to 0.15625
- source_area: int32 [32, 12], replicated, may hold values from 0 to 31, as said below
- delays: int32 [32, 12], replicated, may hold values from 1 to 3
- live_blocks: int32 [32], replicated, may hold values from 8 to 64, as said below
Outputs:
- activity: float32 [32, 64, 32, 128], P('area', 'pop')
The draws below stay inside these ranges and needn't reach their ends.
Inputs may be any that keep to these rules, and one draw needn't show every extreme that they name: `source_area`: the 12 source areas of an area are distinct and differ from the area itself. `live_blocks`: some area is fully populated and some has 8 populated blocks.
All inputs are finite; a program needn't handle non-finite values.
Results may differ from the reference program's by a relative error of at most 0.0014.
Values may be sent and summed in bfloat16 or wider, within the bound.
No kernel may reach another device: no remote copies, remote signals or barrier semaphores. Data moves between devices by JAX's collectives and lax.ppermute only.
A program may use at most 64 MiB of HBM per device.

```python
import math
import jax
import jax.numpy as jnp
from jax import lax

B = 128
BLK_DEV = 8
TR = 32
K = 32
E = 12
SEND_DEV = 2
DMAX = 3
STEPS = 10
AREAS = 32
BLOCKS = 64


def draw_source_area(key, part):
    scores = jax.random.randint(key, (AREAS, AREAS - 1), 0, 2 ** 30)
    offsets = jnp.argsort(scores, axis=1, stable=True)[:, :E].astype(jnp.int32) + 1
    return ((jnp.arange(AREAS, dtype=jnp.int32)[:, None] + offsets) % AREAS).astype(jnp.int32)


def draw_live_blocks(key, part):
    first_key, second_key, third_key = jax.random.split(key, 3)
    counted = jax.random.randint(first_key, (AREAS,), BLOCKS // 8, BLOCKS + 1)
    full_area = jax.random.randint(second_key, (), 0, AREAS)
    offset_area = jax.random.randint(third_key, (), 1, AREAS)
    thin_area = (full_area + offset_area) % AREAS
    counted = counted.at[full_area].set(BLOCKS).at[thin_area].set(BLOCKS // 8)
    return counted.astype(jnp.int32)


def set_ends(values, rng, smallest, largest):
    extent = values.shape
    place = [jax.random.randint(jax.random.fold_in(rng, axis), (), 0, extent[axis]) for axis in range(len(extent))]
    values = values.at[tuple(place)].set(smallest)
    longest = extent.index(max(extent))
    place[longest] = (place[longest] + 1) % extent[longest]
    return values.at[tuple(place)].set(largest)


def level_of(stream_key, shape, pieces, least, high):
    factor_of, own = 1.0, jax.random.fold_in(stream_key, 6)
    for axis_at, shards_of in pieces:
        steps = jnp.exp(jax.random.uniform(jax.random.fold_in(own, axis_at), (shards_of,), jnp.float32, least / len(pieces), high / len(pieces)))
        factor_of = factor_of * jnp.repeat(steps, shape[axis_at] // shards_of).reshape([-1 if axis == axis_at else 1 for axis in range(len(shape))])
    return factor_of


def normal_values(own_key, extent, deviation, most, cuts=(), held_as=jnp.bfloat16):
    gain = level_of(own_key, extent, cuts, -0.22, 0.18) if cuts else 1.0
    values = jax.random.normal(own_key, extent, jnp.float32) * deviation * gain
    return jnp.minimum(jnp.maximum(values, -most), most).astype(held_as)


def setup_inputs(seed: int = 0) -> dict:
    keys = jax.random.split(jax.random.key(seed), 11)
    history = jnp.clip(jax.random.uniform(keys[0], (DMAX + 1, AREAS, BLOCKS, TR, B), jnp.float32, -1.0, 1.0) * level_of(keys[0], (DMAX + 1, AREAS, BLOCKS, TR, B), ((1, 32), (2, 8)), -0.4, 0.0), -1.0, 1.0).astype(jnp.bfloat16)
    external = normal_values(keys[1], (AREAS, BLOCKS, TR, B), 1.0, 6.0, ((0, 32), (1, 8)))
    leak_rate = jnp.clip(jnp.exp(math.log(1.0) - 2.9957323 * jax.random.uniform(keys[2], (AREAS, BLOCKS, B), jnp.float32) ** level_of(keys[2], (AREAS, BLOCKS, B), ((0, 32), (1, 8)), -0.2, 0.2)), 0.05, 1.0)
    intra_index = set_ends(jax.random.randint(keys[3], (AREAS, BLOCKS, K), 0, BLOCKS), jax.random.fold_in(keys[3], 1), 0, BLOCKS - 1).astype(jnp.int32)
    intra_weight = normal_values(keys[4], (AREAS, BLOCKS, K, B, B), (K * B) ** -0.5, 0.09375, ((0, 32), (1, 8)))
    inter_pick = set_ends(jax.random.randint(keys[5], (AREAS, BLOCKS, E), 0, SEND_DEV), jax.random.fold_in(keys[5], 1), 0, SEND_DEV - 1).astype(jnp.int32)
    inter_weight = normal_values(keys[6], (AREAS, BLOCKS, E, B, B), (E * B) ** -0.5, 0.15625, ((0, 32), (1, 8)))
    source_area = draw_source_area(jax.random.fold_in(keys[10], 71), 0)
    delays = set_ends(jax.random.randint(keys[8], (AREAS, E), 1, DMAX + 1), jax.random.fold_in(keys[8], 1), 1, DMAX).astype(jnp.int32)
    live_blocks = draw_live_blocks(jax.random.fold_in(keys[10], 71), 0)
    return dict(history=history, external=external, leak_rate=leak_rate, intra_index=intra_index, intra_weight=intra_weight, inter_pick=inter_pick, inter_weight=inter_weight, source_area=source_area, delays=delays, live_blocks=live_blocks)


def reference(history, external, leak_rate, intra_index, intra_weight, inter_pick, inter_weight, source_area, delays, live_blocks):
    block_ids = jnp.arange(BLOCKS, dtype=jnp.int32)
    alive = (block_ids[None, :] < live_blocks[:, None]).astype(jnp.float32)
    alive_cells = alive[:, :, None, None]
    rate_hist = (history.astype(jnp.float32) * alive_cells[None]).astype(jnp.bfloat16)
    activity = rate_hist[0].astype(jnp.float32)
    section = (block_ids // BLK_DEV) * BLK_DEV
    leak_cells = leak_rate[:, :, None, :]
    drive_ext = external.astype(jnp.float32)

    def area_current(area_id, rate_hist):
        tile_rows = rate_hist[0, area_id][intra_index[area_id]]
        inner_term = jnp.einsum('rkji,rktj->rti', intra_weight[area_id].astype(jnp.float32), tile_rows.astype(jnp.float32))
        edge_rows = rate_hist[delays[area_id][None, :], source_area[area_id][None, :], section[:, None] + inter_pick[area_id]]
        outer_term = jnp.einsum('rkji,rktj->rti', inter_weight[area_id].astype(jnp.float32), edge_rows.astype(jnp.float32))
        return inner_term + outer_term

    for turn in range(STEPS):
        current = lax.map(lambda area_id: area_current(area_id, rate_hist), jnp.arange(AREAS, dtype=jnp.int32))
        drive_term = jnp.tanh(current + drive_ext)
        activity = alive_cells * ((1.0 - leak_cells) * activity + leak_cells * drive_term)
        rate_now = activity.astype(jnp.bfloat16)
        rate_hist = jnp.concatenate([rate_now[None], rate_hist[:-1]], 0)
    return activity
```

```python
import functools
import jax
import jax.numpy as jnp
from jax import lax
from jax.experimental import pallas as pl
from jax.experimental.pallas import tpu as pltpu
from jax.sharding import PartitionSpec as P

SEND_DEV = 2
STEPS = 10
DMAX = 3

VMEM = pl.BlockSpec(memory_space=pltpu.VMEM)
SMEM = pl.BlockSpec(memory_space=pltpu.SMEM)


def tile_product(rows, weights):
    lhs = jnp.concatenate(rows, axis=1)
    rhs = weights.reshape(lhs.shape[1], weights.shape[-1])
    return lax.dot_general(
        lhs, rhs, (((1,), (0,)), ((), ())), preferred_element_type=jnp.float32
    )


def choose(delay_ref, recent_ref, chosen_ref):
    for area in range(chosen_ref.shape[0]):
        chosen_ref[area] = recent_ref[delay_ref[area]]


def first_kernel(count_ref, delay_ref, history_ref, activity_ref, spread_ref, now_ref, next_ref, recent_ref, older_ref):
    blocks = activity_ref.shape[0]
    count = count_ref[0]
    for block in range(blocks):
        alive = jnp.where(block < count, 1.0, 0.0)
        rates = (history_ref[0, block].astype(jnp.float32) * alive).astype(jnp.bfloat16)
        activity_ref[block] = rates.astype(jnp.float32)
        for pop in range(spread_ref.shape[0]):
            spread_ref[pop, block] = rates
    for block in range(SEND_DEV):
        alive = jnp.where(block < count, 1.0, 0.0)
        for age in range(DMAX + 1):
            rates = (history_ref[age, block].astype(jnp.float32) * alive).astype(jnp.bfloat16)
            older_ref[age, block] = rates
            if age < DMAX:
                recent_ref[age, block] = rates
    choose(delay_ref, older_ref.at[1:], now_ref)
    choose(delay_ref, older_ref, next_ref)


def inter_kernel(source_ref, pick_ref, received_ref, weight_ref, external_ref, out_ref):
    blocks, edges = weight_ref.shape[:2]

    def body(block, carry):
        rows = [received_ref[source_ref[e], pick_ref[block, e]] for e in range(edges)]
        total = tile_product(rows, weight_ref[block])
        out_ref[block] = total + external_ref[block].astype(jnp.float32)
        return carry

    lax.fori_loop(0, blocks, body, 0)


def intra_kernel(last, choosing, count_ref, delay_ref, index_ref, rates_ref, weight_ref, outer_ref, leak_ref, activity_ref, *refs):
    if choosing:
        recent_in_ref, activity_out_ref, spread_ref, recent_ref, chosen_ref = refs
    elif last:
        (activity_out_ref,) = refs
    else:
        activity_out_ref, spread_ref = refs
    blocks, tiles = weight_ref.shape[:2]
    count = count_ref[0]

    def body(block, carry):
        rows = [rates_ref[index_ref[block, k]] for k in range(tiles)]
        current = tile_product(rows, weight_ref[block]) + outer_ref[block]
        leak = leak_ref[block]
        alive = jnp.where(block < count, 1.0, 0.0)
        new = alive * ((1.0 - leak) * activity_ref[block] + leak * jnp.tanh(current))
        activity_out_ref[block] = new
        if not last:
            rates = new.astype(jnp.bfloat16)
            for pop in range(spread_ref.shape[0]):
                spread_ref[pop, block] = rates
        return carry

    lax.fori_loop(0, blocks, body, 0)
    if choosing:
        recent_ref[0] = spread_ref[0, :SEND_DEV]
        for age in range(1, DMAX):
            recent_ref[age] = recent_in_ref[age - 1]
        choose(delay_ref, recent_ref, chosen_ref)


def shards(
    history,
    external,
    leak_rate,
    intra_index,
    intra_weight,
    inter_pick,
    inter_weight,
    source_area,
    delays,
    live_blocks,
):
    area_pos = lax.axis_index("area")
    pop_pos = lax.axis_index("pop")
    areas = lax.axis_size("area")
    pops = lax.axis_size("pop")
    history = history[:, 0]
    blocks, conds, units = history.shape[1:]
    tiles = intra_index.shape[2]
    edges = inter_pick.shape[2]
    count = (live_blocks[area_pos] - pop_pos * blocks)[None]
    delay_to = jnp.sum(jnp.where(source_area == area_pos, delays, 0), axis=1)
    delay_to = jnp.maximum(delay_to, 1) - 1
    my_source = source_area[area_pos]
    index = intra_index[0]
    pick = inter_pick[0]
    w_intra = intra_weight[0]
    w_inter = inter_weight[0]
    ext = external[0]
    leak = leak_rate[0][:, None, :]

    f32, bf16 = jnp.float32, jnp.bfloat16
    activity_t = jax.ShapeDtypeStruct((blocks, conds, units), f32)
    spread_t = jax.ShapeDtypeStruct((pops, blocks, conds, units), bf16)
    recent_t = jax.ShapeDtypeStruct((DMAX, SEND_DEV, conds, units), bf16)
    chosen_t = jax.ShapeDtypeStruct((areas, SEND_DEV, conds, units), bf16)
    params = pltpu.CompilerParams(vmem_limit_bytes=24 * 2**20)

    activity, spread, now, nxt, recent = pl.pallas_call(
        first_kernel,
        out_shape=(activity_t, spread_t, chosen_t, chosen_t, recent_t),
        in_specs=[SMEM, SMEM, VMEM],
        out_specs=(VMEM,) * 5,
        scratch_shapes=[pltpu.VMEM((DMAX + 1, SEND_DEV, conds, units), bf16)],
        compiler_params=params,
    )(count, delay_to, history)

    inter = pl.pallas_call(
        inter_kernel,
        out_shape=activity_t,
        in_specs=[SMEM, SMEM, VMEM, VMEM, VMEM],
        out_specs=VMEM,
        compiler_params=params,
        cost_estimate=pl.CostEstimate(
            flops=2 * blocks * edges * conds * units * units,
            bytes_accessed=2 * blocks * edges * units * units,
            transcendentals=0,
        ),
    )

    def exchange(x, axis):
        return lax.all_to_all(x, axis, split_axis=0, concat_axis=0, tiled=True)

    received = [exchange(now, "area"), exchange(nxt, "area")]
    for step in range(STEPS):
        rates = exchange(spread, "pop").reshape(pops * blocks, conds, units)
        outer = inter(my_source, pick, received[step], w_inter, ext)
        last = step == STEPS - 1
        choosing = step + 2 < STEPS
        outs = (activity_t,) if last else (activity_t, spread_t)
        if choosing:
            outs += (recent_t, chosen_t)
        got = pl.pallas_call(
            functools.partial(intra_kernel, last, choosing),
            out_shape=outs,
            in_specs=[SMEM] * 3 + [VMEM] * (6 if choosing else 5),
            out_specs=(VMEM,) * len(outs),
            compiler_params=params,
            cost_estimate=pl.CostEstimate(
                flops=2 * blocks * tiles * conds * units * units,
                bytes_accessed=2 * blocks * tiles * units * units,
                transcendentals=blocks * conds * units,
            ),
        )(count, delay_to, index, rates, w_intra, outer, leak, activity, *((recent,) if choosing else ()))
        activity = got[0]
        if not last:
            spread = got[1]
        if choosing:
            recent = got[2]
            received.append(exchange(got[3], "area"))
    return activity[None]


def solution(mesh):
    placed = (
        P(None, "area", "pop", None, None),
        P("area", "pop", None, None),
        P("area", "pop", None),
        P("area", "pop", None),
        P("area", "pop", None, None, None),
        P("area", "pop", None),
        P("area", "pop", None, None, None),
        P(),
        P(),
        P(),
    )
    return jax.shard_map(
        shards, mesh=mesh, in_specs=placed, out_specs=P("area", "pop", None, None), check_vma=False
    )
```

```python
import functools
import jax
import jax.numpy as jnp
from jax import lax
from jax.experimental import pallas as pl
from jax.experimental.pallas import tpu as pltpu
from jax.sharding import PartitionSpec as P

SEND_DEV = 2
STEPS = 10
DMAX = 3
SPAN = 2

VMEM = pl.BlockSpec(memory_space=pltpu.VMEM)
SMEM = pl.BlockSpec(memory_space=pltpu.SMEM)


def tile_product(rows, weights):
    lhs = jnp.concatenate(rows, axis=1)
    rhs = weights.reshape(lhs.shape[1], weights.shape[-1])
    return lax.dot_general(
        lhs, rhs, (((1,), (0,)), ((), ())), preferred_element_type=jnp.float32
    )


def choose(delay_ref, older_ref, chosen_ref):
    for area in range(chosen_ref.shape[0]):
        delay = delay_ref[area]
        chosen_ref[area, :SEND_DEV] = older_ref[delay]
        chosen_ref[area, SEND_DEV:] = older_ref[delay - 1]


def first_kernel(count_ref, delay_ref, history_ref, activity_ref, spread_ref, chosen_ref, recent_ref, older_ref):
    blocks = activity_ref.shape[0]
    count = count_ref[0]
    for block in range(blocks):
        alive = jnp.where(block < count, 1.0, 0.0)
        rates = (history_ref[0, block].astype(jnp.float32) * alive).astype(jnp.bfloat16)
        activity_ref[block] = rates.astype(jnp.float32)
        for pop in range(spread_ref.shape[0]):
            spread_ref[pop, block] = rates
    for block in range(SEND_DEV):
        alive = jnp.where(block < count, 1.0, 0.0)
        for age in range(DMAX + 1):
            rates = (history_ref[age, block].astype(jnp.float32) * alive).astype(jnp.bfloat16)
            older_ref[age, block] = rates
            if age < DMAX:
                recent_ref[age, block] = rates
    choose(delay_ref, older_ref, chosen_ref)


def step_kernel(
    phase, last, choosing,
    count_ref, delay_ref, source_ref, pick_ref, index_ref,
    rates_ref, received_ref, intra_ref, inter_ref, external_ref, leak_ref, activity_ref, recent_ref,
    *refs,
):
    if last:
        (activity_out_ref,) = refs
    elif choosing:
        activity_out_ref, spread_ref, recent_out_ref, chosen_ref, older_ref = refs
    else:
        activity_out_ref, spread_ref, recent_out_ref = refs
    blocks, tiles = intra_ref.shape[:2]
    edges = inter_ref.shape[1]
    count = count_ref[0]

    def body(block, carry):
        rows = [received_ref[source_ref[e], SEND_DEV * phase + pick_ref[block, e]] for e in range(edges)]
        current = tile_product(rows, inter_ref[block])
        rows = [rates_ref[index_ref[block, k]] for k in range(tiles)]
        current += tile_product(rows, intra_ref[block])
        leak = leak_ref[block]
        alive = jnp.where(block < count, 1.0, 0.0)
        driven = jnp.tanh(current + external_ref[block].astype(jnp.float32))
        new = alive * ((1.0 - leak) * activity_ref[block] + leak * driven)
        activity_out_ref[block] = new
        if not last:
            rates = new.astype(jnp.bfloat16)
            for pop in range(spread_ref.shape[0]):
                spread_ref[pop, block] = rates
        return carry

    lax.fori_loop(0, blocks, body, 0)
    if not last:
        recent_out_ref[0] = spread_ref[0, :SEND_DEV]
        for age in range(1, DMAX):
            recent_out_ref[age] = recent_ref[age - 1]
    if choosing:
        older_ref[0] = spread_ref[0, :SEND_DEV]
        for age in range(DMAX):
            older_ref[age + 1] = recent_ref[age]
        choose(delay_ref, older_ref, chosen_ref)


def shards(
    history,
    external,
    leak_rate,
    intra_index,
    intra_weight,
    inter_pick,
    inter_weight,
    source_area,
    delays,
    live_blocks,
):
    area_pos = lax.axis_index("area")
    pop_pos = lax.axis_index("pop")
    areas = lax.axis_size("area")
    pops = lax.axis_size("pop")
    history = history[:, 0]
    blocks, conds, units = history.shape[1:]
    tiles = intra_index.shape[2]
    edges = inter_pick.shape[2]
    count = (live_blocks[area_pos] - pop_pos * blocks)[None]
    delay_to = jnp.sum(jnp.where(source_area == area_pos, delays, 0), axis=1)
    delay_to = jnp.maximum(delay_to, 1)
    my_source = source_area[area_pos]
    leak = leak_rate[0][:, None, :]

    f32, bf16 = jnp.float32, jnp.bfloat16
    activity_t = jax.ShapeDtypeStruct((blocks, conds, units), f32)
    spread_t = jax.ShapeDtypeStruct((pops, blocks, conds, units), bf16)
    recent_t = jax.ShapeDtypeStruct((DMAX, SEND_DEV, conds, units), bf16)
    chosen_t = jax.ShapeDtypeStruct((areas, SPAN * SEND_DEV, conds, units), bf16)
    older = pltpu.VMEM((DMAX + 1, SEND_DEV, conds, units), bf16)
    params = pltpu.CompilerParams(vmem_limit_bytes=4 * 2**20)

    activity, spread, chosen, recent = pl.pallas_call(
        first_kernel,
        out_shape=(activity_t, spread_t, chosen_t, recent_t),
        in_specs=[SMEM, SMEM, VMEM],
        out_specs=(VMEM,) * 4,
        scratch_shapes=[older],
        compiler_params=params,
    )(count, delay_to, history)

    def exchange(x, axis):
        return lax.all_to_all(x, axis, split_axis=0, concat_axis=0, tiled=True)

    products = blocks * (tiles + edges) * units * units
    for step in range(STEPS):
        phase = step % SPAN
        if phase == 0:
            received = exchange(chosen, "area")
        rates = exchange(spread, "pop").reshape(pops * blocks, conds, units)
        last = step == STEPS - 1
        choosing = phase == SPAN - 1 and not last
        outs = (activity_t,) if last else (activity_t, spread_t, recent_t)
        if choosing:
            outs += (chosen_t,)
        got = pl.pallas_call(
            functools.partial(step_kernel, phase, last, choosing),
            out_shape=outs,
            in_specs=[SMEM] * 5 + [VMEM] * 8,
            out_specs=(VMEM,) * len(outs),
            scratch_shapes=[older] if choosing else [],
            compiler_params=params,
            cost_estimate=pl.CostEstimate(
                flops=2 * products * conds,
                bytes_accessed=2 * products,
                transcendentals=blocks * conds * units,
            ),
        )(
            count, delay_to, my_source, inter_pick[0], intra_index[0],
            rates, received, intra_weight[0], inter_weight[0], external[0], leak, activity, recent,
        )
        activity = got[0]
        if not last:
            spread, recent = got[1:3]
        if choosing:
            chosen = got[3]
    return activity[None]


def solution(mesh):
    placed = (
        P(None, "area", "pop", None, None),
        P("area", "pop", None, None),
        P("area", "pop", None),
        P("area", "pop", None),
        P("area", "pop", None, None, None),
        P("area", "pop", None),
        P("area", "pop", None, None, None),
        P(),
        P(),
        P(),
    )
    return jax.shard_map(
        shards, mesh=mesh, in_specs=placed, out_specs=P("area", "pop", None, None), check_vma=False
    )
```

```python
import functools
import jax
import jax.numpy as jnp
from jax import lax
from jax.experimental import pallas as pl
from jax.experimental.pallas import tpu as pltpu
from jax.sharding import PartitionSpec as P

SEND_DEV = 2
STEPS = 10
DMAX = 3
SPAN = 2

VMEM = pl.BlockSpec(memory_space=pltpu.VMEM)
SMEM = pl.BlockSpec(memory_space=pltpu.SMEM)
ANY = pl.BlockSpec(memory_space=pl.ANY)
HBM = pl.BlockSpec(memory_space=pltpu.HBM)


def tile_product(rows, weights):
    lhs = jnp.concatenate(rows, axis=1)
    rhs = weights.reshape(lhs.shape[1], weights.shape[-1])
    return lax.dot_general(
        lhs, rhs, (((1,), (0,)), ((), ())), preferred_element_type=jnp.float32
    )


def choose(delay_ref, older_ref, chosen_ref):
    for area in range(chosen_ref.shape[0]):
        delay = delay_ref[area]
        chosen_ref[area, :SEND_DEV] = older_ref[delay]
        chosen_ref[area, SEND_DEV:] = older_ref[delay - 1]


def first_kernel(count_ref, delay_ref, history_ref, activity_ref, spread_ref, chosen_ref, recent_ref, older_ref):
    blocks = activity_ref.shape[0]
    count = count_ref[0]
    for block in range(blocks):
        alive = jnp.where(block < count, 1.0, 0.0)
        rates = (history_ref[0, block].astype(jnp.float32) * alive).astype(jnp.bfloat16)
        activity_ref[block] = rates.astype(jnp.float32)
        for pop in range(spread_ref.shape[0]):
            spread_ref[pop, block] = rates
    for block in range(SEND_DEV):
        alive = jnp.where(block < count, 1.0, 0.0)
        for age in range(DMAX + 1):
            rates = (history_ref[age, block].astype(jnp.float32) * alive).astype(jnp.bfloat16)
            older_ref[age, block] = rates
            if age < DMAX:
                recent_ref[age, block] = rates
    choose(delay_ref, older_ref, chosen_ref)


def step_kernel(
    phase, last, choosing,
    count_ref, delay_ref, source_ref, pick_ref, index_ref,
    rates_hbm, received_hbm, intra_hbm, inter_hbm, external_ref, leak_ref, activity_ref, recent_ref,
    *refs,
):
    outs, scratch = refs[:-9], refs[-9:]
    rates_ref, received_ref, intra_ref, inter_ref, rates_sem, received_sem, intra_sem, inter_sem, outer_ref = scratch
    chosen_ref = None
    if last:
        (activity_out_ref,) = outs
    elif choosing:
        activity_out_ref, spread_ref, recent_out_ref, chosen_hbm, older_ref, chosen_ref, chosen_sem = outs
    else:
        activity_out_ref, spread_ref, recent_out_ref = outs
    blocks, tiles = intra_ref.shape[:2]
    edges = inter_ref.shape[1]
    count = count_ref[0]

    def received_copy(e):
        return pltpu.make_async_copy(
            received_hbm.at[source_ref[e], pl.ds(SEND_DEV * phase, SEND_DEV)], received_ref.at[e], received_sem.at[e]
        )

    def intra_copy(block):
        return pltpu.make_async_copy(intra_hbm.at[block], intra_ref.at[block], intra_sem.at[block])

    def inter_copy(block):
        return pltpu.make_async_copy(inter_hbm.at[block], inter_ref.at[block], inter_sem.at[block])

    rates_copy = pltpu.make_async_copy(rates_hbm, rates_ref, rates_sem)
    for e in range(edges):
        received_copy(e).start()
    for block in range(blocks):
        inter_copy(block).start()
    rates_copy.start()
    for block in range(blocks):
        intra_copy(block).start()
    for e in range(edges):
        received_copy(e).wait()

    def outer_body(block, carry):
        inter_copy(block).wait()
        rows = [received_ref[e, pick_ref[block, e]] for e in range(edges)]
        outer_ref[block] = tile_product(rows, inter_ref[block]) + external_ref[block].astype(jnp.float32)
        return carry

    lax.fori_loop(0, blocks, outer_body, 0)
    rates_copy.wait()

    def body(block, carry):
        intra_copy(block).wait()
        rows = [rates_ref[index_ref[block, k]] for k in range(tiles)]
        current = tile_product(rows, intra_ref[block]) + outer_ref[block]
        leak = leak_ref[block]
        alive = jnp.where(block < count, 1.0, 0.0)
        new = alive * ((1.0 - leak) * activity_ref[block] + leak * jnp.tanh(current))
        activity_out_ref[block] = new
        if not last:
            rates = new.astype(jnp.bfloat16)
            for pop in range(spread_ref.shape[0]):
                spread_ref[pop, block] = rates
        return carry

    lax.fori_loop(0, SEND_DEV, body, 0)
    if choosing:
        older_ref[0] = spread_ref[0, :SEND_DEV]
        for age in range(DMAX):
            older_ref[age + 1] = recent_ref[age]
        choose(delay_ref, older_ref, chosen_ref)
        chosen_copy = pltpu.make_async_copy(chosen_ref, chosen_hbm, chosen_sem)
        chosen_copy.start()
    lax.fori_loop(SEND_DEV, blocks, body, 0)
    if not last:
        recent_out_ref[0] = spread_ref[0, :SEND_DEV]
        for age in range(1, DMAX):
            recent_out_ref[age] = recent_ref[age - 1]
    if choosing:
        chosen_copy.wait()


def shards(
    history,
    external,
    leak_rate,
    intra_index,
    intra_weight,
    inter_pick,
    inter_weight,
    source_area,
    delays,
    live_blocks,
):
    area_pos = lax.axis_index("area")
    pop_pos = lax.axis_index("pop")
    areas = lax.axis_size("area")
    pops = lax.axis_size("pop")
    history = history[:, 0]
    blocks, conds, units = history.shape[1:]
    tiles = intra_index.shape[2]
    edges = inter_pick.shape[2]
    count = (live_blocks[area_pos] - pop_pos * blocks)[None]
    delay_to = jnp.sum(jnp.where(source_area == area_pos, delays, 0), axis=1)
    delay_to = jnp.maximum(delay_to, 1)
    my_source = source_area[area_pos]
    leak = leak_rate[0][:, None, :]

    f32, bf16 = jnp.float32, jnp.bfloat16
    activity_t = jax.ShapeDtypeStruct((blocks, conds, units), f32)
    spread_t = [
        jax.ShapeDtypeStruct((1, blocks, conds, units), bf16),
        jax.ShapeDtypeStruct((pops, blocks, conds, units), bf16),
    ]
    recent_t = jax.ShapeDtypeStruct((DMAX, SEND_DEV, conds, units), bf16)
    chosen_t = jax.ShapeDtypeStruct((areas, SPAN * SEND_DEV, conds, units), bf16)
    older = pltpu.VMEM((DMAX + 1, SEND_DEV, conds, units), bf16)
    params = pltpu.CompilerParams(vmem_limit_bytes=50 * 2**20)

    activity, spread, chosen, recent = pl.pallas_call(
        first_kernel,
        out_shape=(activity_t, spread_t[0], chosen_t, recent_t),
        in_specs=[SMEM, SMEM, VMEM],
        out_specs=(VMEM,) * 4,
        scratch_shapes=[older],
        compiler_params=params,
    )(count, delay_to, history)

    def exchange(x, axis):
        return lax.all_to_all(x, axis, split_axis=0, concat_axis=0, tiled=True)

    half = pops // 2
    strided = [list(range(parity, pops, 2)) for parity in range(2)]
    paired = [[2 * pair, 2 * pair + 1] for pair in range(half)]

    def gather(x):
        x = lax.all_gather(x, "pop", axis=0, axis_index_groups=strided, tiled=True)
        return lax.all_gather(x, "pop", axis=0, axis_index_groups=paired, tiled=True)

    index = intra_index[0]
    owner, place = index // blocks, index % blocks
    indices = [((owner % 2) * half + owner // 2) * blocks + place, index]

    chosen_scratch = pltpu.VMEM(chosen_t.shape, bf16)
    scratch = [
        pltpu.VMEM((pops * blocks, conds, units), bf16),
        pltpu.VMEM((edges, SEND_DEV, conds, units), bf16),
        pltpu.VMEM((blocks, tiles, units, units), bf16),
        pltpu.VMEM((blocks, edges, units, units), bf16),
        pltpu.SemaphoreType.DMA,
        pltpu.SemaphoreType.DMA((edges,)),
        pltpu.SemaphoreType.DMA((blocks,)),
        pltpu.SemaphoreType.DMA((blocks,)),
        pltpu.VMEM((blocks, conds, units), f32),
    ]
    products = blocks * (tiles + edges) * units * units
    for step in range(STEPS):
        phase = step % SPAN
        if phase == 0:
            received = exchange(chosen, "area")
            rates = gather(spread)
        else:
            rates = exchange(spread, "pop")
        rates = rates.reshape(pops * blocks, conds, units)
        last = step == STEPS - 1
        choosing = phase == SPAN - 1 and not last
        outs = (activity_t,) if last else (activity_t, spread_t[1 - phase], recent_t)
        if choosing:
            outs += (chosen_t,)
        got = pl.pallas_call(
            functools.partial(step_kernel, phase, last, choosing),
            out_shape=outs,
            in_specs=[SMEM] * 5 + [ANY, ANY, HBM, HBM] + [VMEM] * 4,
            out_specs=(VMEM,) * min(len(outs), 3) + (ANY,) * choosing,
            scratch_shapes=([older, chosen_scratch, pltpu.SemaphoreType.DMA] if choosing else []) + scratch,
            compiler_params=params,
            cost_estimate=pl.CostEstimate(
                flops=2 * products * conds,
                bytes_accessed=2 * products,
                transcendentals=blocks * conds * units,
            ),
        )(
            count, delay_to, my_source, inter_pick[0], indices[phase],
            rates, received, intra_weight[0], inter_weight[0], external[0], leak, activity, recent,
        )
        activity = got[0]
        if not last:
            spread, recent = got[1:3]
        if choosing:
            chosen = got[3]
    return activity[None]


def solution(mesh):
    placed = (
        P(None, "area", "pop", None, None),
        P("area", "pop", None, None),
        P("area", "pop", None),
        P("area", "pop", None),
        P("area", "pop", None, None, None),
        P("area", "pop", None),
        P("area", "pop", None, None, None),
        P(),
        P(),
        P(),
    )
    return jax.shard_map(
        shards, mesh=mesh, in_specs=placed, out_specs=P("area", "pop", None, None), check_vma=False
    )
```

```python
import functools
import jax
import jax.numpy as jnp
from jax import lax
from jax.experimental import pallas as pl
from jax.experimental.pallas import tpu as pltpu
from jax.sharding import PartitionSpec as P

SEND_DEV = 2
STEPS = 10
DMAX = 3
SPAN = 2

VMEM = pl.BlockSpec(memory_space=pltpu.VMEM)
SMEM = pl.BlockSpec(memory_space=pltpu.SMEM)
ANY = pl.BlockSpec(memory_space=pl.ANY)
HBM = pl.BlockSpec(memory_space=pltpu.HBM)


def tile_product(rows, weights):
    lhs = jnp.concatenate(rows, axis=1)
    rhs = weights.reshape(lhs.shape[1], weights.shape[-1])
    return lax.dot_general(
        lhs, rhs, (((1,), (0,)), ((), ())), preferred_element_type=jnp.float32
    )


def choose(delay_ref, older_ref, chosen_ref):
    for area in range(chosen_ref.shape[0]):
        delay = delay_ref[area]
        chosen_ref[area, :SEND_DEV] = older_ref[delay]
        chosen_ref[area, SEND_DEV:] = older_ref[delay - 1]


def first_kernel(
    delay_ref, source_ref, live_ref, index_ref, history_hbm, *refs
):
    moved = (len(refs) - 14) // 2
    sources, outs, places = refs[:moved], refs[moved : moved + 6], refs[moved + 6 : 2 * moved + 6]
    activity_ref, rates_ref, chosen_hbm, recent_ref, table_ref, gathered_index_ref = outs
    scratch = refs[2 * moved + 6 :]
    history_ref, tail_ref, older_ref, chosen_ref, history_sem, tail_sem, chosen_sem, moved_sem = scratch
    blocks = activity_ref.shape[0]
    edges = source_ref.shape[0]
    area = lax.axis_index("area")
    pops = lax.axis_size("pop")
    tail_copy = pltpu.make_async_copy(history_hbm.at[:, pl.ds(0, SEND_DEV)], tail_ref, tail_sem)
    history_copy = pltpu.make_async_copy(history_hbm.at[0], history_ref, history_sem)
    tail_copy.start()
    history_copy.start()
    copies = [pltpu.make_async_copy(sources[i], places[i], moved_sem.at[i]) for i in range(moved)]
    for copy in copies:
        copy.start()
    count = live_ref[area] - lax.axis_index("pop") * blocks
    table_ref[0] = count
    for e in range(edges):
        table_ref[1 + e] = source_ref[e, area]
    owner, place = index_ref[...] // blocks, index_ref[...] % blocks
    gathered_index_ref[...] = ((owner % 2) * (pops // 2) + owner // 2) * blocks + place
    tail_copy.wait()
    for block in range(SEND_DEV):
        alive = jnp.where(block < count, 1.0, 0.0)
        for age in range(DMAX + 1):
            rates = (tail_ref[age, block].astype(jnp.float32) * alive).astype(jnp.bfloat16)
            older_ref[age, block] = rates
            if age < DMAX:
                recent_ref[age, block] = rates
    choose(delay_ref, older_ref, chosen_ref)
    chosen_copy = pltpu.make_async_copy(chosen_ref, chosen_hbm, chosen_sem)
    chosen_copy.start()
    history_copy.wait()
    for block in range(blocks):
        alive = jnp.where(block < count, 1.0, 0.0)
        rates = (history_ref[block].astype(jnp.float32) * alive).astype(jnp.bfloat16)
        activity_ref[block] = rates.astype(jnp.float32)
        rates_ref[0, block] = rates
    for copy in copies:
        copy.wait()
    chosen_copy.wait()


def step_kernel(
    phase, last, choosing,
    table_any, delay_any, pick_any, index_any,
    rates_any, received_any, intra_hbm, inter_hbm, external_ref, leak_ref, activity_ref, recent_ref,
    *refs,
):
    table_ref, delay_ref, pick_ref, index_ref, table_sem, rates_ref, received_ref, intra_ref, inter_ref = refs[:9]
    outer_ref, rates_sem, received_sem, intra_sem, inter_sem = refs[9:14]
    outs = list(refs[14:])
    activity_out_ref = outs.pop(0)
    if not last:
        spread_ref, recent_out_ref = outs.pop(0), outs.pop(0)
    if choosing:
        chosen_hbm, older_ref, chosen_ref, chosen_sem = outs
    blocks, tiles = intra_ref.shape[:2]
    edges = inter_ref.shape[1]

    def received_copy(e):
        return pltpu.make_async_copy(
            received_any.at[table_ref[1 + e], pl.ds(SEND_DEV * phase, SEND_DEV)], received_ref.at[e], received_sem.at[e]
        )

    def intra_copy(block):
        return pltpu.make_async_copy(intra_hbm.at[block], intra_ref.at[block], intra_sem.at[block])

    def inter_copy(block):
        return pltpu.make_async_copy(inter_hbm.at[block], inter_ref.at[block], inter_sem.at[block])

    tables = [(table_any, table_ref), (pick_any, pick_ref), (index_any, index_ref)]
    if choosing:
        tables.append((delay_any, delay_ref))
    table_copies = [pltpu.make_async_copy(src, dst, table_sem.at[i]) for i, (src, dst) in enumerate(tables)]
    rates_copy = pltpu.make_async_copy(rates_any, rates_ref, rates_sem)
    for copy in table_copies:
        copy.start()
    for block in range(blocks):
        inter_copy(block).start()
    rates_copy.start()
    for block in range(blocks):
        intra_copy(block).start()
    table_copies[0].wait()
    for e in range(edges):
        received_copy(e).start()
    for copy in table_copies[1:]:
        copy.wait()
    count = table_ref[0]
    for e in range(edges):
        received_copy(e).wait()

    def outer_body(block, carry):
        inter_copy(block).wait()
        rows = [received_ref[e, pick_ref[block, e]] for e in range(edges)]
        outer_ref[block] = tile_product(rows, inter_ref[block]) + external_ref[block].astype(jnp.float32)
        return carry

    lax.fori_loop(0, blocks, outer_body, 0)
    rates_copy.wait()

    def body(block, carry):
        intra_copy(block).wait()
        rows = [rates_ref[index_ref[block, k]] for k in range(tiles)]
        current = tile_product(rows, intra_ref[block]) + outer_ref[block]
        leak = leak_ref[pl.ds(block, 1), :]
        alive = jnp.where(block < count, 1.0, 0.0)
        new = alive * ((1.0 - leak) * activity_ref[block] + leak * jnp.tanh(current))
        activity_out_ref[block] = new
        if not last:
            rates = new.astype(jnp.bfloat16)
            for pop in range(spread_ref.shape[0]):
                spread_ref[pop, block] = rates
        return carry

    lax.fori_loop(0, SEND_DEV, body, 0)
    if choosing:
        older_ref[0] = spread_ref[0, :SEND_DEV]
        for age in range(DMAX):
            older_ref[age + 1] = recent_ref[age]
        choose(delay_ref, older_ref, chosen_ref)
        chosen_copy = pltpu.make_async_copy(chosen_ref, chosen_hbm, chosen_sem)
        chosen_copy.start()
    lax.fori_loop(SEND_DEV, blocks, body, 0)
    if not last:
        recent_out_ref[0] = spread_ref[0, :SEND_DEV]
        for age in range(1, DMAX):
            recent_out_ref[age] = recent_ref[age - 1]
    if choosing:
        chosen_copy.wait()


def ordered_kernel(n_in, n_out, n_common, kernel):
    def run(*refs):
        ins, outs, scratch = refs[:n_in], refs[n_in : n_in + n_out], refs[n_in + n_out :]
        kernel(*ins, *scratch[:n_common], *outs, *scratch[n_common:])

    return run


def shards(
    history,
    external,
    leak_rate,
    intra_index,
    intra_weight,
    inter_pick,
    inter_weight,
    source_area,
    delays,
    live_blocks,
):
    areas = lax.axis_size("area")
    pops = lax.axis_size("pop")
    history = history[:, 0]
    blocks, conds, units = history.shape[1:]
    tiles = intra_index.shape[2]
    edges = inter_pick.shape[2]

    f32, bf16, i32 = jnp.float32, jnp.bfloat16, jnp.int32
    shape = jax.ShapeDtypeStruct
    activity_t = shape((blocks, conds, units), f32)
    spread_t = [shape((pops, blocks, conds, units), bf16), shape((1, blocks, conds, units), bf16)]
    recent_t = shape((DMAX, SEND_DEV, conds, units), bf16)
    chosen_t = shape((areas, SPAN * SEND_DEV, conds, units), bf16)
    older = pltpu.VMEM((DMAX + 1, SEND_DEV, conds, units), bf16)
    chosen_scratch = pltpu.VMEM(chosen_t.shape, bf16)
    one = pltpu.SemaphoreType.DMA
    params = pltpu.CompilerParams(vmem_limit_bytes=50 * 2**20)

    area_pos = lax.axis_index("area")
    delay_to = jnp.sum(jnp.where(source_area == area_pos, delays, 0), axis=1)
    delay_to = jnp.maximum(delay_to, 1)
    moved = [external[0], leak_rate[0], inter_pick[0], intra_index[0]]
    activity, spread, chosen, recent, table, gathered_index, *moved = pl.pallas_call(
        first_kernel,
        out_shape=(
            activity_t, spread_t[1], chosen_t, recent_t,
            shape((1 + edges,), i32), shape((blocks, tiles), i32),
            *(shape(x.shape, x.dtype) for x in moved),
        ),
        in_specs=[SMEM] * 3 + [VMEM, ANY] + [ANY] * len(moved),
        out_specs=(VMEM, VMEM, ANY, VMEM, SMEM, VMEM) + (VMEM,) * len(moved),
        scratch_shapes=[
            pltpu.VMEM((blocks, conds, units), bf16),
            pltpu.VMEM((DMAX + 1, SEND_DEV, conds, units), bf16),
            older, chosen_scratch, one, one, one, pltpu.SemaphoreType.DMA((len(moved),)),
        ],
        compiler_params=pltpu.CompilerParams(vmem_limit_bytes=50 * 2**20),
    )(delay_to, source_area.T, live_blocks, intra_index[0], history, *moved)
    external, leak, pick, index = moved
    inter = inter_weight[0]

    def exchange(x, axis):
        return lax.all_to_all(x, axis, split_axis=0, concat_axis=0, tiled=True)

    strided = [list(range(parity, pops, 2)) for parity in range(2)]
    paired = [[2 * pair, 2 * pair + 1] for pair in range(pops // 2)]

    def gather(x):
        x = lax.all_gather(x, "pop", axis=0, axis_index_groups=strided, tiled=True)
        return lax.all_gather(x, "pop", axis=0, axis_index_groups=paired, tiled=True)

    common = [
        pltpu.SMEM((1 + edges,), i32),
        pltpu.SMEM((areas,), i32),
        pltpu.SMEM((blocks, edges), i32),
        pltpu.SMEM((blocks, tiles), i32),
        pltpu.SemaphoreType.DMA((4,)),
        pltpu.VMEM((pops * blocks, conds, units), bf16),
        pltpu.VMEM((edges, SEND_DEV, conds, units), bf16),
        pltpu.VMEM((blocks, tiles, units, units), bf16),
        pltpu.VMEM((blocks, edges, units, units), bf16),
        pltpu.VMEM((blocks, conds, units), f32),
        one,
        pltpu.SemaphoreType.DMA((edges,)),
        pltpu.SemaphoreType.DMA((blocks,)),
        pltpu.SemaphoreType.DMA((blocks,)),
    ]
    products = blocks * (tiles + edges) * units * units
    for step in range(STEPS):
        phase = step % SPAN
        last = step == STEPS - 1
        choosing = phase == SPAN - 1 and not last
        if phase == 0:
            received = exchange(chosen, "area")
            rates = gather(spread)
        else:
            rates = exchange(spread, "pop")
        outs, places, scratch = [activity_t], [VMEM], []
        if not last:
            outs += [spread_t[phase], recent_t]
            places += [VMEM, VMEM]
        if choosing:
            outs.append(chosen_t)
            places.append(ANY)
            scratch += [older, chosen_scratch, one]
        ins = (
            table, delay_to, pick, index if phase else gathered_index,
            rates.reshape(pops * blocks, conds, units), received, intra_weight[0], inter,
            external, leak, activity, recent,
        )
        got = pl.pallas_call(
            ordered_kernel(len(ins), len(outs), len(common), functools.partial(step_kernel, phase, last, choosing)),
            out_shape=tuple(outs),
            in_specs=[ANY] * 6 + [HBM] * 2 + [VMEM] * 4,
            out_specs=tuple(places),
            scratch_shapes=common + scratch,
            compiler_params=params,
            cost_estimate=pl.CostEstimate(
                flops=2 * products * conds,
                bytes_accessed=2 * products,
                transcendentals=blocks * conds * units,
            ),
        )(*ins)
        activity = got[0]
        if not last:
            spread, recent = got[1:3]
        if choosing:
            chosen = got[3]
    return activity[None]


def solution(mesh):
    placed = (
        P(None, "area", "pop", None, None),
        P("area", "pop", None, None),
        P("area", "pop", None),
        P("area", "pop", None),
        P("area", "pop", None, None, None),
        P("area", "pop", None),
        P("area", "pop", None, None, None),
        P(),
        P(),
        P(),
    )
    return jax.shard_map(
        shards, mesh=mesh, in_specs=placed, out_specs=P("area", "pop", None, None), check_vma=False
    )
```

```python
import functools
import jax
import jax.numpy as jnp
from jax import lax
from jax.experimental import pallas as pl
from jax.experimental.pallas import tpu as pltpu
from jax.sharding import PartitionSpec as P

SEND_DEV = 2
STEPS = 10
DMAX = 3
KEPT = 3
SPAN = 2

VMEM = pl.BlockSpec(memory_space=pltpu.VMEM)
SMEM = pl.BlockSpec(memory_space=pltpu.SMEM)
ANY = pl.BlockSpec(memory_space=pl.ANY)
HBM = pl.BlockSpec(memory_space=pltpu.HBM)


def tile_product(rows, weights):
    lhs = jnp.concatenate(rows, axis=1)
    rhs = weights.reshape(lhs.shape[1], weights.shape[-1])
    return lax.dot_general(
        lhs, rhs, (((1,), (0,)), ((), ())), preferred_element_type=jnp.float32
    )


def choose(delay_ref, older_ref, chosen_ref):
    for area in range(chosen_ref.shape[0]):
        delay = delay_ref[area]
        chosen_ref[area, :SEND_DEV] = older_ref[delay]
        chosen_ref[area, SEND_DEV:] = older_ref[delay - 1]


def first_kernel(
    delay_ref, source_ref, live_ref, index_ref, history_hbm, *refs
):
    moved = (len(refs) - 14) // 2
    sources, outs, places = refs[:moved], refs[moved : moved + 6], refs[moved + 6 : 2 * moved + 6]
    activity_ref, rates_ref, chosen_hbm, recent_ref, table_ref, gathered_index_ref = outs
    scratch = refs[2 * moved + 6 :]
    history_ref, tail_ref, older_ref, chosen_ref, history_sem, tail_sem, chosen_sem, moved_sem = scratch
    blocks = activity_ref.shape[0]
    edges = source_ref.shape[0]
    area = lax.axis_index("area")
    pops = lax.axis_size("pop")
    tail_copy = pltpu.make_async_copy(history_hbm.at[:, pl.ds(0, SEND_DEV)], tail_ref, tail_sem)
    history_copy = pltpu.make_async_copy(history_hbm.at[0], history_ref, history_sem)
    tail_copy.start()
    history_copy.start()
    copies = [pltpu.make_async_copy(sources[i], places[i], moved_sem.at[i]) for i in range(moved)]
    for copy in copies:
        copy.start()
    count = live_ref[area] - lax.axis_index("pop") * blocks
    table_ref[0] = count
    for e in range(edges):
        table_ref[1 + e] = source_ref[e, area]
    owner, place = index_ref[...] // blocks, index_ref[...] % blocks
    gathered_index_ref[...] = ((owner % 2) * (pops // 2) + owner // 2) * blocks + place
    tail_copy.wait()
    for block in range(SEND_DEV):
        alive = jnp.where(block < count, 1.0, 0.0)
        for age in range(DMAX + 1):
            rates = (tail_ref[age, block].astype(jnp.float32) * alive).astype(jnp.bfloat16)
            older_ref[age, block] = rates
            if age < DMAX:
                recent_ref[age, block] = rates
    choose(delay_ref, older_ref, chosen_ref)
    chosen_copy = pltpu.make_async_copy(chosen_ref, chosen_hbm, chosen_sem)
    chosen_copy.start()
    history_copy.wait()
    for block in range(blocks):
        alive = jnp.where(block < count, 1.0, 0.0)
        rates = (history_ref[block].astype(jnp.float32) * alive).astype(jnp.bfloat16)
        activity_ref[block] = rates.astype(jnp.float32)
        rates_ref[0, block] = rates
    for copy in copies:
        copy.wait()
    chosen_copy.wait()


def step_kernel(
    phase, last, choosing,
    table_any, delay_any, pick_any, index_any,
    rates_any, received_any, intra_hbm, inter_hbm, kept_ref, external_ref, leak_ref, activity_ref, recent_ref,
    *refs,
):
    table_ref, delay_ref, pick_ref, index_ref, table_sem, rates_ref, received_ref, intra_ref, inter_ref = refs[:9]
    outer_ref, rates_sem, received_sem, intra_sem, inter_sem = refs[9:14]
    outs = list(refs[14:])
    activity_out_ref = outs.pop(0)
    if not last:
        spread_ref, recent_out_ref = outs.pop(0), outs.pop(0)
    if choosing:
        chosen_hbm, older_ref, chosen_ref, chosen_sem = outs
    blocks, tiles = intra_ref.shape[:2]
    edges = inter_ref.shape[1]
    kept = kept_ref.shape[0]

    def received_copy(e):
        return pltpu.make_async_copy(
            received_any.at[table_ref[1 + e], pl.ds(SEND_DEV * phase, SEND_DEV)], received_ref.at[e], received_sem.at[e]
        )

    def intra_copy(block):
        return pltpu.make_async_copy(intra_hbm.at[block], intra_ref.at[block], intra_sem.at[block])

    def inter_copy(block):
        return pltpu.make_async_copy(inter_hbm.at[block], inter_ref.at[block - kept], inter_sem.at[block - kept])

    tables = [(table_any, table_ref), (pick_any, pick_ref), (index_any, index_ref)]
    if choosing:
        tables.append((delay_any, delay_ref))
    table_copies = [pltpu.make_async_copy(src, dst, table_sem.at[i]) for i, (src, dst) in enumerate(tables)]
    rates_copy = pltpu.make_async_copy(rates_any, rates_ref, rates_sem)
    for copy in table_copies:
        copy.start()
    for block in range(kept, blocks):
        inter_copy(block).start()
    rates_copy.start()
    for block in range(blocks):
        intra_copy(block).start()
    table_copies[0].wait()
    for e in range(edges):
        received_copy(e).start()
    for copy in table_copies[1:]:
        copy.wait()
    count = table_ref[0]
    for e in range(edges):
        received_copy(e).wait()

    def outer(block, weights):
        rows = [received_ref[e, pick_ref[block, e]] for e in range(edges)]
        outer_ref[block] = tile_product(rows, weights) + external_ref[block].astype(jnp.float32)

    for block in range(kept):
        outer(block, kept_ref[block])
    for block in range(kept, blocks):
        inter_copy(block).wait()
        outer(block, inter_ref[block - kept])
    rates_copy.wait()

    def advance(block):
        intra_copy(block).wait()
        rows = [rates_ref[index_ref[block, k]] for k in range(tiles)]
        current = tile_product(rows, intra_ref[block]) + outer_ref[block]
        leak = leak_ref[pl.ds(block, 1), :]
        alive = jnp.where(block < count, 1.0, 0.0)
        new = alive * ((1.0 - leak) * activity_ref[block] + leak * jnp.tanh(current))
        activity_out_ref[block] = new
        if not last:
            rates = new.astype(jnp.bfloat16)
            for pop in range(spread_ref.shape[0]):
                spread_ref[pop, block] = rates

    for block in range(SEND_DEV):
        advance(block)
    if choosing:
        older_ref[0] = spread_ref[0, :SEND_DEV]
        for age in range(DMAX):
            older_ref[age + 1] = recent_ref[age]
        choose(delay_ref, older_ref, chosen_ref)
        chosen_copy = pltpu.make_async_copy(chosen_ref, chosen_hbm, chosen_sem)
        chosen_copy.start()
    for block in range(SEND_DEV, blocks):
        advance(block)
    if not last:
        recent_out_ref[0] = spread_ref[0, :SEND_DEV]
        for age in range(1, DMAX):
            recent_out_ref[age] = recent_ref[age - 1]
    if choosing:
        chosen_copy.wait()


def ordered_kernel(n_in, n_out, n_common, kernel):
    def run(*refs):
        ins, outs, scratch = refs[:n_in], refs[n_in : n_in + n_out], refs[n_in + n_out :]
        kernel(*ins, *scratch[:n_common], *outs, *scratch[n_common:])

    return run


def shards(
    history,
    external,
    leak_rate,
    intra_index,
    intra_weight,
    inter_pick,
    inter_weight,
    source_area,
    delays,
    live_blocks,
):
    areas = lax.axis_size("area")
    pops = lax.axis_size("pop")
    history = history[:, 0]
    blocks, conds, units = history.shape[1:]
    tiles = intra_index.shape[2]
    edges = inter_pick.shape[2]

    f32, bf16, i32 = jnp.float32, jnp.bfloat16, jnp.int32
    shape = jax.ShapeDtypeStruct
    activity_t = shape((blocks, conds, units), f32)
    spread_t = [shape((pops, blocks, conds, units), bf16), shape((1, blocks, conds, units), bf16)]
    recent_t = shape((DMAX, SEND_DEV, conds, units), bf16)
    chosen_t = shape((areas, SPAN * SEND_DEV, conds, units), bf16)
    older = pltpu.VMEM((DMAX + 1, SEND_DEV, conds, units), bf16)
    chosen_scratch = pltpu.VMEM(chosen_t.shape, bf16)
    one = pltpu.SemaphoreType.DMA
    params = pltpu.CompilerParams(vmem_limit_bytes=49 * 2**20)

    area_pos = lax.axis_index("area")
    delay_to = jnp.sum(jnp.where(source_area == area_pos, delays, 0), axis=1)
    delay_to = jnp.maximum(delay_to, 1)
    moved = [external[0], leak_rate[0], inter_pick[0], intra_index[0]]
    activity, spread, chosen, recent, table, gathered_index, *moved = pl.pallas_call(
        first_kernel,
        out_shape=(
            activity_t, spread_t[1], chosen_t, recent_t,
            shape((1 + edges,), i32), shape((blocks, tiles), i32),
            *(shape(x.shape, x.dtype) for x in moved),
        ),
        in_specs=[SMEM] * 3 + [VMEM, ANY] + [ANY] * len(moved),
        out_specs=(VMEM, VMEM, ANY, VMEM, SMEM, VMEM) + (VMEM,) * len(moved),
        scratch_shapes=[
            pltpu.VMEM((blocks, conds, units), bf16),
            pltpu.VMEM((DMAX + 1, SEND_DEV, conds, units), bf16),
            older, chosen_scratch, one, one, one, pltpu.SemaphoreType.DMA((len(moved),)),
        ],
        compiler_params=pltpu.CompilerParams(vmem_limit_bytes=50 * 2**20),
    )(delay_to, source_area.T, live_blocks, intra_index[0], history, *moved)
    external, leak, pick, index = moved
    inter = inter_weight[0]

    def exchange(x, axis):
        return lax.all_to_all(x, axis, split_axis=0, concat_axis=0, tiled=True)

    strided = [list(range(parity, pops, 2)) for parity in range(2)]
    paired = [[2 * pair, 2 * pair + 1] for pair in range(pops // 2)]

    def gather(x):
        x = lax.all_gather(x, "pop", axis=0, axis_index_groups=strided, tiled=True)
        return lax.all_gather(x, "pop", axis=0, axis_index_groups=paired, tiled=True)

    common = [
        pltpu.SMEM((1 + edges,), i32),
        pltpu.SMEM((areas,), i32),
        pltpu.SMEM((blocks, edges), i32),
        pltpu.SMEM((blocks, tiles), i32),
        pltpu.SemaphoreType.DMA((4,)),
        pltpu.VMEM((pops * blocks, conds, units), bf16),
        pltpu.VMEM((edges, SEND_DEV, conds, units), bf16),
        pltpu.VMEM((blocks, tiles, units, units), bf16),
        pltpu.VMEM((blocks - KEPT, edges, units, units), bf16),
        pltpu.VMEM((blocks, conds, units), f32),
        one,
        pltpu.SemaphoreType.DMA((edges,)),
        pltpu.SemaphoreType.DMA((blocks,)),
        pltpu.SemaphoreType.DMA((blocks - KEPT,)),
    ]
    products = blocks * (tiles + edges) * units * units
    for step in range(STEPS):
        phase = step % SPAN
        last = step == STEPS - 1
        choosing = phase == SPAN - 1 and not last
        if phase == 0:
            received = exchange(chosen, "area")
            rates = gather(spread)
        else:
            rates = exchange(spread, "pop")
        outs, places, scratch = [activity_t], [VMEM], []
        if not last:
            outs += [spread_t[phase], recent_t]
            places += [VMEM, VMEM]
        if choosing:
            outs.append(chosen_t)
            places.append(ANY)
            scratch += [older, chosen_scratch, one]
        ins = (
            table, delay_to, pick, index if phase else gathered_index,
            rates.reshape(pops * blocks, conds, units), received, intra_weight[0], inter, inter[:KEPT],
            external, leak, activity, recent,
        )
        got = pl.pallas_call(
            ordered_kernel(len(ins), len(outs), len(common), functools.partial(step_kernel, phase, last, choosing)),
            out_shape=tuple(outs),
            in_specs=[ANY] * 6 + [HBM] * 2 + [VMEM] * 5,
            out_specs=tuple(places),
            scratch_shapes=common + scratch,
            compiler_params=params,
            cost_estimate=pl.CostEstimate(
                flops=2 * products * conds,
                bytes_accessed=2 * products,
                transcendentals=blocks * conds * units,
            ),
        )(*ins)
        activity = got[0]
        if not last:
            spread, recent = got[1:3]
        if choosing:
            chosen = got[3]
    return activity[None]


def solution(mesh):
    placed = (
        P(None, "area", "pop", None, None),
        P("area", "pop", None, None),
        P("area", "pop", None),
        P("area", "pop", None),
        P("area", "pop", None, None, None),
        P("area", "pop", None),
        P("area", "pop", None, None, None),
        P(),
        P(),
        P(),
    )
    return jax.shard_map(
        shards, mesh=mesh, in_specs=placed, out_specs=P("area", "pop", None, None), check_vma=False
    )
```

```python
import functools
import jax
import jax.numpy as jnp
from jax import lax
from jax.experimental import pallas as pl
from jax.experimental.pallas import tpu as pltpu
from jax.sharding import PartitionSpec as P

SEND_DEV = 2
STEPS = 10
DMAX = 3
KEPT = 3
SPAN = 2

VMEM = pl.BlockSpec(memory_space=pltpu.VMEM)
SMEM = pl.BlockSpec(memory_space=pltpu.SMEM)
ANY = pl.BlockSpec(memory_space=pl.ANY)
HBM = pl.BlockSpec(memory_space=pltpu.HBM)


def tile_product(rows, weights):
    lhs = jnp.concatenate(rows, axis=1)
    rhs = weights.reshape(lhs.shape[1], weights.shape[-1])
    return lax.dot_general(
        lhs, rhs, (((1,), (0,)), ((), ())), preferred_element_type=jnp.float32
    )


def choose(delay_ref, older_ref, chosen_ref):
    for area in range(chosen_ref.shape[0]):
        delay = delay_ref[area]
        chosen_ref[area, :SEND_DEV] = older_ref[delay]
        chosen_ref[area, SEND_DEV:] = older_ref[delay - 1]


def first_kernel(
    delay_ref, source_ref, live_ref, index_ref, history_hbm, *refs
):
    moved = (len(refs) - 14) // 2
    sources, outs, places = refs[:moved], refs[moved : moved + 6], refs[moved + 6 : 2 * moved + 6]
    activity_ref, rates_ref, chosen_hbm, recent_ref, table_ref, gathered_index_ref = outs
    scratch = refs[2 * moved + 6 :]
    history_ref, tail_ref, older_ref, chosen_ref, history_sem, tail_sem, chosen_sem, moved_sem = scratch
    blocks = activity_ref.shape[0]
    edges = source_ref.shape[0]
    area = lax.axis_index("area")
    pops = lax.axis_size("pop")
    tail_copy = pltpu.make_async_copy(history_hbm.at[:, pl.ds(0, SEND_DEV)], tail_ref, tail_sem)
    history_copy = pltpu.make_async_copy(history_hbm.at[0], history_ref, history_sem)
    tail_copy.start()
    history_copy.start()
    copies = [pltpu.make_async_copy(sources[i], places[i], moved_sem.at[i]) for i in range(moved)]
    for copy in copies:
        copy.start()
    count = live_ref[area] - lax.axis_index("pop") * blocks
    table_ref[0] = count
    for e in range(edges):
        table_ref[1 + e] = source_ref[e, area]
    owner, place = index_ref[...] // blocks, index_ref[...] % blocks
    gathered_index_ref[...] = ((owner % 2) * (pops // 2) + owner // 2) * blocks + place
    tail_copy.wait()
    for block in range(SEND_DEV):
        alive = jnp.where(block < count, 1.0, 0.0)
        for age in range(DMAX + 1):
            rates = (tail_ref[age, block].astype(jnp.float32) * alive).astype(jnp.bfloat16)
            older_ref[age, block] = rates
            if age < DMAX:
                recent_ref[age, block] = rates
    choose(delay_ref, older_ref, chosen_ref)
    chosen_copy = pltpu.make_async_copy(chosen_ref, chosen_hbm, chosen_sem)
    chosen_copy.start()
    history_copy.wait()
    for block in range(blocks):
        alive = jnp.where(block < count, 1.0, 0.0)
        rates = (history_ref[block].astype(jnp.float32) * alive).astype(jnp.bfloat16)
        activity_ref[block] = rates.astype(jnp.float32)
        rates_ref[0, block] = rates
    for copy in copies:
        copy.wait()
    chosen_copy.wait()


def step_kernel(
    phase, last, choosing,
    table_any, delay_any, pick_any, index_any,
    rates_any, received_any, intra_hbm, inter_hbm, kept_ref, external_ref, leak_ref, activity_ref, recent_ref,
    *refs,
):
    table_ref, delay_ref, pick_ref, index_ref, table_sem, rates_ref, received_ref, intra_ref, inter_ref = refs[:9]
    outer_ref, rates_sem, received_sem, intra_sem, inter_sem = refs[9:14]
    outs = list(refs[14:])
    activity_out_ref = outs.pop(0)
    if not last:
        spread_ref, recent_out_ref = outs.pop(0), outs.pop(0)
    if choosing:
        chosen_hbm, older_ref, chosen_ref, chosen_sem = outs
    blocks, tiles = intra_ref.shape[:2]
    edges = inter_ref.shape[1]
    kept = kept_ref.shape[0]

    def received_copy(e):
        return pltpu.make_async_copy(
            received_any.at[table_ref[1 + e], pl.ds(SEND_DEV * phase, SEND_DEV)], received_ref.at[e], received_sem.at[e]
        )

    def intra_copy(block):
        return pltpu.make_async_copy(intra_hbm.at[block], intra_ref.at[block], intra_sem.at[block])

    def inter_copy(block):
        return pltpu.make_async_copy(inter_hbm.at[block], inter_ref.at[block - kept], inter_sem.at[block - kept])

    tables = [(table_any, table_ref), (pick_any, pick_ref), (index_any, index_ref)]
    if choosing:
        tables.append((delay_any, delay_ref))
    table_copies = [pltpu.make_async_copy(src, dst, table_sem.at[i]) for i, (src, dst) in enumerate(tables)]
    rates_copy = pltpu.make_async_copy(rates_any, rates_ref, rates_sem)
    for copy in table_copies:
        copy.start()
    for block in range(kept, blocks):
        inter_copy(block).start()
    rates_copy.start()
    for block in range(blocks):
        intra_copy(block).start()
    table_copies[0].wait()
    for e in range(edges):
        received_copy(e).start()
    for copy in table_copies[1:]:
        copy.wait()
    count = table_ref[0]
    for e in range(edges):
        received_copy(e).wait()

    def outer(block, weights):
        rows = [received_ref[e, pick_ref[block, e]] for e in range(edges)]
        outer_ref[block] = tile_product(rows, weights) + external_ref[block].astype(jnp.float32)

    for block in range(kept):
        outer(block, kept_ref[block])
    for block in range(kept, blocks):
        inter_copy(block).wait()
        outer(block, inter_ref[block - kept])
    rates_copy.wait()

    def advance(block):
        intra_copy(block).wait()
        rows = [rates_ref[index_ref[block, k]] for k in range(tiles)]
        current = tile_product(rows, intra_ref[block]) + outer_ref[block]
        leak = leak_ref[pl.ds(block, 1), :]
        alive = jnp.where(block < count, 1.0, 0.0)
        new = alive * ((1.0 - leak) * activity_ref[block] + leak * jnp.tanh(current))
        activity_out_ref[block] = new
        if not last:
            rates = new.astype(jnp.bfloat16)
            for pop in range(spread_ref.shape[0]):
                spread_ref[pop, block] = rates

    for block in range(SEND_DEV):
        advance(block)
    if choosing:
        older_ref[0] = spread_ref[0, :SEND_DEV]
        for age in range(DMAX):
            older_ref[age + 1] = recent_ref[age]
        choose(delay_ref, older_ref, chosen_ref)
        chosen_copy = pltpu.make_async_copy(chosen_ref, chosen_hbm, chosen_sem)
        chosen_copy.start()
    for block in range(SEND_DEV, blocks):
        advance(block)
    if not last:
        recent_out_ref[0] = spread_ref[0, :SEND_DEV]
        for age in range(1, DMAX):
            recent_out_ref[age] = recent_ref[age - 1]
    if choosing:
        chosen_copy.wait()


def ordered_kernel(n_in, n_out, n_common, kernel):
    def run(*refs):
        ins, outs, scratch = refs[:n_in], refs[n_in : n_in + n_out], refs[n_in + n_out :]
        kernel(*ins, *scratch[:n_common], *outs, *scratch[n_common:])

    return run


def shards(
    history,
    external,
    leak_rate,
    intra_index,
    intra_weight,
    inter_pick,
    inter_weight,
    source_area,
    delays,
    live_blocks,
):
    areas = lax.axis_size("area")
    pops = lax.axis_size("pop")
    history = history[:, 0]
    blocks, conds, units = history.shape[1:]
    tiles = intra_index.shape[2]
    edges = inter_pick.shape[2]

    f32, bf16, i32 = jnp.float32, jnp.bfloat16, jnp.int32
    shape = jax.ShapeDtypeStruct
    activity_t = shape((blocks, conds, units), f32)
    spread_t = [shape((pops, blocks, conds, units), bf16), shape((1, blocks, conds, units), bf16)]
    recent_t = shape((DMAX, SEND_DEV, conds, units), bf16)
    chosen_t = shape((areas, SPAN * SEND_DEV, conds, units), bf16)
    older = pltpu.VMEM((DMAX + 1, SEND_DEV, conds, units), bf16)
    chosen_scratch = pltpu.VMEM(chosen_t.shape, bf16)
    one = pltpu.SemaphoreType.DMA
    params = pltpu.CompilerParams(vmem_limit_bytes=49 * 2**20)

    area_pos = lax.axis_index("area")
    delay_to = jnp.sum(jnp.where(source_area == area_pos, delays, 0), axis=1)
    delay_to = jnp.maximum(delay_to, 1)
    moved = [external[0], leak_rate[0], inter_pick[0], intra_index[0]]
    activity, spread, chosen, recent, table, gathered_index, *moved = pl.pallas_call(
        first_kernel,
        out_shape=(
            activity_t, spread_t[1], chosen_t, recent_t,
            shape((1 + edges,), i32), shape((blocks, tiles), i32),
            *(shape(x.shape, x.dtype) for x in moved),
        ),
        in_specs=[SMEM] * 3 + [VMEM, ANY] + [ANY] * len(moved),
        out_specs=(VMEM, VMEM, ANY, VMEM, SMEM, VMEM) + (VMEM,) * len(moved),
        scratch_shapes=[
            pltpu.VMEM((blocks, conds, units), bf16),
            pltpu.VMEM((DMAX + 1, SEND_DEV, conds, units), bf16),
            older, chosen_scratch, one, one, one, pltpu.SemaphoreType.DMA((len(moved),)),
        ],
        compiler_params=pltpu.CompilerParams(vmem_limit_bytes=56 * 2**20),
    )(delay_to, source_area.T, live_blocks, intra_index[0], history, *moved)
    external, leak, pick, index = moved
    inter = inter_weight[0]

    def exchange(x, axis):
        return lax.all_to_all(x, axis, split_axis=0, concat_axis=0, tiled=True)

    strided = [list(range(parity, pops, 2)) for parity in range(2)]
    paired = [[2 * pair, 2 * pair + 1] for pair in range(pops // 2)]

    def gather(x):
        x = lax.all_gather(x, "pop", axis=0, axis_index_groups=strided, tiled=True)
        return lax.all_gather(x, "pop", axis=0, axis_index_groups=paired, tiled=True)

    common = [
        pltpu.SMEM((1 + edges,), i32),
        pltpu.SMEM((areas,), i32),
        pltpu.SMEM((blocks, edges), i32),
        pltpu.SMEM((blocks, tiles), i32),
        pltpu.SemaphoreType.DMA((4,)),
        pltpu.VMEM((pops * blocks, conds, units), bf16),
        pltpu.VMEM((edges, SEND_DEV, conds, units), bf16),
        pltpu.VMEM((blocks, tiles, units, units), bf16),
        pltpu.VMEM((blocks - KEPT, edges, units, units), bf16),
        pltpu.VMEM((blocks, conds, units), f32),
        one,
        pltpu.SemaphoreType.DMA((edges,)),
        pltpu.SemaphoreType.DMA((blocks,)),
        pltpu.SemaphoreType.DMA((blocks - KEPT,)),
    ]
    products = blocks * (tiles + edges) * units * units
    for step in range(STEPS):
        phase = step % SPAN
        last = step == STEPS - 1
        choosing = phase == SPAN - 1 and not last
        if phase == 0:
            received = exchange(chosen, "area")
            rates = gather(spread)
        else:
            rates = exchange(spread, "pop")
        outs, places, scratch = [activity_t], [VMEM], []
        if not last:
            outs += [spread_t[phase], recent_t]
            places += [VMEM, VMEM]
        if choosing:
            outs.append(chosen_t)
            places.append(ANY)
            scratch += [older, chosen_scratch, one]
        ins = (
            table, delay_to, pick, index if phase else gathered_index,
            rates.reshape(pops * blocks, conds, units), received, intra_weight[0], inter, inter[:KEPT],
            external, leak, activity, recent,
        )
        got = pl.pallas_call(
            ordered_kernel(len(ins), len(outs), len(common), functools.partial(step_kernel, phase, last, choosing)),
            out_shape=tuple(outs),
            in_specs=[ANY] * 6 + [HBM] * 2 + [VMEM] * 5,
            out_specs=tuple(places),
            scratch_shapes=common + scratch,
            compiler_params=params,
            cost_estimate=pl.CostEstimate(
                flops=2 * products * conds,
                bytes_accessed=2 * products,
                transcendentals=blocks * conds * units,
            ),
        )(*ins)
        activity = got[0]
        if not last:
            spread, recent = got[1:3]
        if choosing:
            chosen = got[3]
    return activity[None]


def solution(mesh):
    placed = (
        P(None, "area", "pop", None, None),
        P("area", "pop", None, None),
        P("area", "pop", None),
        P("area", "pop", None),
        P("area", "pop", None, None, None),
        P("area", "pop", None),
        P("area", "pop", None, None, None),
        P(),
        P(),
        P(),
    )
    return jax.shard_map(
        shards, mesh=mesh, in_specs=placed, out_specs=P("area", "pop", None, None), check_vma=False
    )
```

```python
import functools
import jax
import jax.numpy as jnp
from jax import lax
from jax.experimental import pallas as pl
from jax.experimental.pallas import tpu as pltpu
from jax.sharding import PartitionSpec as P

SEND_DEV = 2
STEPS = 10
DMAX = 3
KEPT = 3
SPAN = 2

VMEM = pl.BlockSpec(memory_space=pltpu.VMEM)
SMEM = pl.BlockSpec(memory_space=pltpu.SMEM)
ANY = pl.BlockSpec(memory_space=pl.ANY)
HBM = pl.BlockSpec(memory_space=pltpu.HBM)


def tile_product(rows, weights):
    lhs = jnp.concatenate(rows, axis=1)
    rhs = weights.reshape(lhs.shape[1], weights.shape[-1])
    return lax.dot_general(
        lhs, rhs, (((1,), (0,)), ((), ())), preferred_element_type=jnp.float32
    )


def choose(delay_ref, older_ref, chosen_ref):
    for area in range(chosen_ref.shape[0]):
        delay = jnp.maximum(delay_ref[area], 1)
        chosen_ref[area, :SEND_DEV] = older_ref[delay]
        chosen_ref[area, SEND_DEV:] = older_ref[delay - 1]


def first_kernel(
    delay_ref, source_ref, live_ref, index_ref, history_hbm, *refs
):
    moved = (len(refs) - 14) // 2
    sources, outs, places = refs[:moved], refs[moved : moved + 6], refs[moved + 6 : 2 * moved + 6]
    activity_ref, rates_ref, chosen_hbm, recent_ref, table_ref, gathered_index_ref = outs
    scratch = refs[2 * moved + 6 :]
    history_ref, tail_ref, older_ref, chosen_ref, history_sem, tail_sem, chosen_sem, moved_sem = scratch
    blocks = activity_ref.shape[0]
    edges = source_ref.shape[0]
    area = lax.axis_index("area")
    pops = lax.axis_size("pop")
    tail_copy = pltpu.make_async_copy(history_hbm.at[:, pl.ds(0, SEND_DEV)], tail_ref, tail_sem)
    history_copy = pltpu.make_async_copy(history_hbm.at[0], history_ref, history_sem)
    tail_copy.start()
    history_copy.start()
    copies = [pltpu.make_async_copy(sources[i], places[i], moved_sem.at[i]) for i in range(moved)]
    for copy in copies:
        copy.start()
    count = live_ref[area] - lax.axis_index("pop") * blocks
    table_ref[0] = count
    for e in range(edges):
        table_ref[1 + e] = source_ref[e, area]
    owner, place = index_ref[...] // blocks, index_ref[...] % blocks
    gathered_index_ref[...] = ((owner % 2) * (pops // 2) + owner // 2) * blocks + place
    tail_copy.wait()
    for block in range(SEND_DEV):
        alive = jnp.where(block < count, 1.0, 0.0)
        for age in range(DMAX + 1):
            rates = (tail_ref[age, block].astype(jnp.float32) * alive).astype(jnp.bfloat16)
            older_ref[age, block] = rates
            if age < DMAX:
                recent_ref[age, block] = rates
    choose(delay_ref, older_ref, chosen_ref)
    chosen_copy = pltpu.make_async_copy(chosen_ref, chosen_hbm, chosen_sem)
    chosen_copy.start()
    history_copy.wait()
    for block in range(blocks):
        alive = jnp.where(block < count, 1.0, 0.0)
        rates = (history_ref[block].astype(jnp.float32) * alive).astype(jnp.bfloat16)
        activity_ref[block] = rates.astype(jnp.float32)
        rates_ref[0, block] = rates
    for copy in copies:
        copy.wait()
    chosen_copy.wait()


def step_kernel(
    phase, last, choosing,
    table_any, delay_any, pick_any, index_any,
    rates_any, received_any, intra_hbm, inter_hbm, kept_ref, external_ref, leak_ref, activity_ref, recent_ref,
    *refs,
):
    table_ref, delay_ref, pick_ref, index_ref, table_sem, rates_ref, received_ref, intra_ref, inter_ref = refs[:9]
    outer_ref, rates_sem, received_sem, intra_sem, inter_sem = refs[9:14]
    outs = list(refs[14:])
    activity_out_ref = outs.pop(0)
    if not last:
        spread_ref, recent_out_ref = outs.pop(0), outs.pop(0)
    if choosing:
        chosen_hbm, older_ref, chosen_ref, chosen_sem = outs
    blocks, tiles = intra_ref.shape[:2]
    edges = inter_ref.shape[1]
    kept = kept_ref.shape[0]

    def received_copy(e):
        return pltpu.make_async_copy(
            received_any.at[table_ref[1 + e], pl.ds(SEND_DEV * phase, SEND_DEV)], received_ref.at[e], received_sem.at[e]
        )

    def intra_copy(block):
        return pltpu.make_async_copy(intra_hbm.at[block], intra_ref.at[block], intra_sem.at[block])

    def inter_copy(block):
        return pltpu.make_async_copy(inter_hbm.at[block], inter_ref.at[block - kept], inter_sem.at[block - kept])

    tables = [(table_any, table_ref), (pick_any, pick_ref), (index_any, index_ref)]
    if choosing:
        tables.append((delay_any, delay_ref))
    table_copies = [pltpu.make_async_copy(src, dst, table_sem.at[i]) for i, (src, dst) in enumerate(tables)]
    rates_copy = pltpu.make_async_copy(rates_any, rates_ref, rates_sem)
    for copy in table_copies:
        copy.start()
    for block in range(kept, blocks):
        inter_copy(block).start()
    rates_copy.start()
    for block in range(blocks):
        intra_copy(block).start()
    table_copies[0].wait()
    for e in range(edges):
        received_copy(e).start()
    for copy in table_copies[1:]:
        copy.wait()
    count = table_ref[0]
    for e in range(edges):
        received_copy(e).wait()

    def outer(block, weights):
        rows = [received_ref[e, pick_ref[block, e]] for e in range(edges)]
        outer_ref[block] = tile_product(rows, weights) + external_ref[block].astype(jnp.float32)

    for block in range(kept):
        outer(block, kept_ref[block])
    for block in range(kept, blocks):
        inter_copy(block).wait()
        outer(block, inter_ref[block - kept])
    rates_copy.wait()

    def advance(block):
        intra_copy(block).wait()
        rows = [rates_ref[index_ref[block, k]] for k in range(tiles)]
        current = tile_product(rows, intra_ref[block]) + outer_ref[block]
        leak = leak_ref[pl.ds(block, 1), :]
        alive = jnp.where(block < count, 1.0, 0.0)
        new = alive * ((1.0 - leak) * activity_ref[block] + leak * jnp.tanh(current))
        activity_out_ref[block] = new
        if not last:
            rates = new.astype(jnp.bfloat16)
            for pop in range(spread_ref.shape[0]):
                spread_ref[pop, block] = rates

    for block in range(SEND_DEV):
        advance(block)
    if choosing:
        older_ref[0] = spread_ref[0, :SEND_DEV]
        for age in range(DMAX):
            older_ref[age + 1] = recent_ref[age]
        choose(delay_ref, older_ref, chosen_ref)
        chosen_copy = pltpu.make_async_copy(chosen_ref, chosen_hbm, chosen_sem)
        chosen_copy.start()
    for block in range(SEND_DEV, blocks):
        advance(block)
    if not last:
        recent_out_ref[0] = spread_ref[0, :SEND_DEV]
        for age in range(1, DMAX):
            recent_out_ref[age] = recent_ref[age - 1]
    if choosing:
        chosen_copy.wait()


def ordered_kernel(n_in, n_out, n_common, kernel):
    def run(*refs):
        ins, outs, scratch = refs[:n_in], refs[n_in : n_in + n_out], refs[n_in + n_out :]
        kernel(*ins, *scratch[:n_common], *outs, *scratch[n_common:])

    return run


def shards(
    history,
    external,
    leak_rate,
    intra_index,
    intra_weight,
    inter_pick,
    inter_weight,
    source_area,
    delays,
    live_blocks,
):
    areas = lax.axis_size("area")
    pops = lax.axis_size("pop")
    history = history[:, 0]
    blocks, conds, units = history.shape[1:]
    tiles = intra_index.shape[2]
    edges = inter_pick.shape[2]

    f32, bf16, i32 = jnp.float32, jnp.bfloat16, jnp.int32
    shape = jax.ShapeDtypeStruct
    activity_t = shape((blocks, conds, units), f32)
    spread_t = [shape((pops, blocks, conds, units), bf16), shape((1, blocks, conds, units), bf16)]
    recent_t = shape((DMAX, SEND_DEV, conds, units), bf16)
    chosen_t = shape((areas, SPAN * SEND_DEV, conds, units), bf16)
    older = pltpu.VMEM((DMAX + 1, SEND_DEV, conds, units), bf16)
    chosen_scratch = pltpu.VMEM(chosen_t.shape, bf16)
    one = pltpu.SemaphoreType.DMA
    params = pltpu.CompilerParams(vmem_limit_bytes=49 * 2**20)

    area_pos = lax.axis_index("area")
    delay_to = jnp.sum(jnp.where(source_area == area_pos, delays, 0), axis=1)
    moved = [external[0], leak_rate[0], inter_pick[0], intra_index[0]]
    activity, spread, chosen, recent, table, gathered_index, *moved = pl.pallas_call(
        first_kernel,
        out_shape=(
            activity_t, spread_t[1], chosen_t, recent_t,
            shape((1 + edges,), i32), shape((blocks, tiles), i32),
            *(shape(x.shape, x.dtype) for x in moved),
        ),
        in_specs=[SMEM] * 3 + [VMEM, ANY] + [ANY] * len(moved),
        out_specs=(VMEM, VMEM, ANY, VMEM, SMEM, VMEM) + (VMEM,) * len(moved),
        scratch_shapes=[
            pltpu.VMEM((blocks, conds, units), bf16),
            pltpu.VMEM((DMAX + 1, SEND_DEV, conds, units), bf16),
            older, chosen_scratch, one, one, one, pltpu.SemaphoreType.DMA((len(moved),)),
        ],
        compiler_params=pltpu.CompilerParams(vmem_limit_bytes=56 * 2**20),
    )(delay_to, source_area.T, live_blocks, intra_index[0], history, *moved)
    external, leak, pick, index = moved
    inter = inter_weight[0]

    def exchange(x, axis):
        return lax.all_to_all(x, axis, split_axis=0, concat_axis=0, tiled=True)

    strided = [list(range(parity, pops, 2)) for parity in range(2)]
    paired = [[2 * pair, 2 * pair + 1] for pair in range(pops // 2)]

    def gather(x):
        x = lax.all_gather(x, "pop", axis=0, axis_index_groups=strided, tiled=True)
        return lax.all_gather(x, "pop", axis=0, axis_index_groups=paired, tiled=True)

    common = [
        pltpu.SMEM((1 + edges,), i32),
        pltpu.SMEM((areas,), i32),
        pltpu.SMEM((blocks, edges), i32),
        pltpu.SMEM((blocks, tiles), i32),
        pltpu.SemaphoreType.DMA((4,)),
        pltpu.VMEM((pops * blocks, conds, units), bf16),
        pltpu.VMEM((edges, SEND_DEV, conds, units), bf16),
        pltpu.VMEM((blocks, tiles, units, units), bf16),
        pltpu.VMEM((blocks - KEPT, edges, units, units), bf16),
        pltpu.VMEM((blocks, conds, units), f32),
        one,
        pltpu.SemaphoreType.DMA((edges,)),
        pltpu.SemaphoreType.DMA((blocks,)),
        pltpu.SemaphoreType.DMA((blocks - KEPT,)),
    ]
    products = blocks * (tiles + edges) * units * units
    for step in range(STEPS):
        phase = step % SPAN
        last = step == STEPS - 1
        choosing = phase == SPAN - 1 and not last
        if phase == 0:
            received = exchange(chosen, "area")
            rates = gather(spread)
        else:
            rates = exchange(spread, "pop")
        outs, places, scratch = [activity_t], [VMEM], []
        if not last:
            outs += [spread_t[phase], recent_t]
            places += [VMEM, VMEM]
        if choosing:
            outs.append(chosen_t)
            places.append(ANY)
            scratch += [older, chosen_scratch, one]
        ins = (
            table, delay_to, pick, index if phase else gathered_index,
            rates.reshape(pops * blocks, conds, units), received, intra_weight[0], inter, inter[:KEPT],
            external, leak, activity, recent,
        )
        got = pl.pallas_call(
            ordered_kernel(len(ins), len(outs), len(common), functools.partial(step_kernel, phase, last, choosing)),
            out_shape=tuple(outs),
            in_specs=[ANY] * 6 + [HBM] * 2 + [VMEM] * 5,
            out_specs=tuple(places),
            scratch_shapes=common + scratch,
            compiler_params=params,
            cost_estimate=pl.CostEstimate(
                flops=2 * products * conds,
                bytes_accessed=2 * products,
                transcendentals=blocks * conds * units,
            ),
        )(*ins)
        activity = got[0]
        if not last:
            spread, recent = got[1:3]
        if choosing:
            chosen = got[3]
    return activity[None]


def solution(mesh):
    placed = (
        P(None, "area", "pop", None, None),
        P("area", "pop", None, None),
        P("area", "pop", None),
        P("area", "pop", None),
        P("area", "pop", None, None, None),
        P("area", "pop", None),
        P("area", "pop", None, None, None),
        P(),
        P(),
        P(),
    )
    return jax.shard_map(
        shards, mesh=mesh, in_specs=placed, out_specs=P("area", "pop", None, None), check_vma=False
    )
```
